32 devices in a mesh: visit: 8 (over y, x, core), row: 4 (over z).
Axes of the slice: x: 2, y: 2, z: 4, core: 2. Of those that a mesh axis runs over, the one named last changes fastest.
Arguments:
- science: float32 [8, 128, 4096], P('visit', 'row'), may hold values from -8 to 8
- basis_kernels: float32 [9, 21, 21], replicated, may hold values from -0.25 to 0.25
- basis_coeffs: float32 [8, 9], P('visit'), may hold values from -2 to 2
- row_starts: int32 [8, 128], P('visit', 'row'), may hold values from -7 to 1
- row_taps: float32 [8, 8, 128], P('visit', None, 'row'), may hold values from -0.2 to 0.45
- col_offsets: int32 [8], P('visit'), may hold values from 0 to 511
- col_starts: int32 [8, 4096], P('visit'), may hold values from -3 to -2
- col_taps: float32 [8, 8, 4096], P('visit'), may hold values from -0.2 to 0.45
- visit_weights: float32 [8], P('visit'), may hold values from 0.25 to 4
- clip_masks: int32 [8, 128, 4096], P('visit', 'row'), may hold values 0 or 1
- decorrelation: float32 [8, 21, 21], P('visit'), may hold values from -0.25 to 0.25
Outputs:
- decorrelated: float32 [8, 128, 4096], P('visit', 'row')
- template: float32 [128, 4096], P('row', 'visit')
The draws below stay inside these ranges and needn't reach their ends.
Inputs may be any that keep to these rules, and one draw needn't show every extreme that they name: Row i of a visit reads matched rows i + row_starts[v, i] to i + row_starts[v, i] + 7.
All inputs are finite; a program needn't handle non-finite values. No bound on the sum of `clip_masks` on one device may be relied on, other than what follows from the above.
Results may differ from the reference program's by a relative error of at most 0.0003.
Values sent between devices are 32-bit elements; how exact they have to be, the bound alone decides.
A program may use at most 64 MiB of HBM per device.

```python
import math
import jax
import jax.numpy as jnp
from jax import lax

W = 4096
KS = 21
NBASIS = 9
TAPS = 8
DITHER = 512
VISITS = 8
H = 128


def place_ends(entries, own_key, least, top_value):
    place = [jax.random.randint(jax.random.fold_in(own_key, axis), (), 0, length) for axis, length in enumerate(entries.shape)]
    main_axis = entries.shape.index(max(entries.shape))
    neighbour = place[:main_axis] + [(place[main_axis] + 1) % entries.shape[main_axis]] + place[main_axis + 1:]
    return entries.at[tuple(place)].set(least).at[tuple(neighbour)].set(top_value)


def block_levels(key, extent, split, smallest, top_value):
    level = 1.0
    for axis_at, shards_of in split:
        steps = jax.random.uniform(jax.random.fold_in(jax.random.fold_in(key, 6), axis_at), (shards_of,), jnp.float32, smallest / len(split), top_value / len(split))
        level = level * jnp.repeat(jnp.exp(steps), extent[axis_at] // shards_of).reshape((-1,) + (1,) * (len(extent) - 1 - axis_at))
    return level


def gaussian(own_key, dims, width, bound, split=(), kind=jnp.bfloat16):
    level = block_levels(own_key, dims, split, -0.22, 0.18) if split else 1.0
    drawn = jax.random.normal(own_key, dims, jnp.float32) * width * level
    return jnp.minimum(jnp.maximum(drawn, -bound), bound).astype(kind)


def setup_inputs(seed: int = 0) -> dict:
    keys = jax.random.split(jax.random.key(seed), 12)
    return {
        "science": gaussian(keys[0], (VISITS, H, W), 1.0, 8.0, ((0, 8), (1, 4)), jnp.float32),
        "basis_kernels": gaussian(keys[1], (NBASIS, KS, KS), (KS * KS) ** -0.5, 0.25, (), jnp.float32),
        "basis_coeffs": gaussian(keys[2], (VISITS, NBASIS), 0.33, 2.0, ((0, 8),), jnp.float32),
        "row_starts": place_ends(jax.random.randint(keys[3], (VISITS, H), -7, 2), jax.random.fold_in(keys[3], 1), -7, 1).astype(jnp.int32),
        "row_taps": jnp.clip(-0.2 + 0.65 * jax.random.uniform(keys[4], (VISITS, TAPS, H), jnp.float32) ** block_levels(keys[4], (VISITS, TAPS, H), ((0, 8), (2, 4)), -0.2, 0.2), -0.2, 0.45),
        "col_offsets": place_ends(jax.random.randint(keys[5], (VISITS,), 0, DITHER), jax.random.fold_in(keys[5], 1), 0, DITHER - 1).astype(jnp.int32),
        "col_starts": place_ends(jax.random.randint(keys[6], (VISITS, W), -3, -1), jax.random.fold_in(keys[6], 1), -3, (-1) - 1).astype(jnp.int32),
        "col_taps": jnp.clip(-0.2 + 0.65 * jax.random.uniform(keys[7], (VISITS, TAPS, W), jnp.float32) ** block_levels(keys[7], (VISITS, TAPS, W), ((0, 8),), -0.2, 0.2), -0.2, 0.45),
        "visit_weights": jnp.clip(jnp.exp(math.log(4.0) - 2.7725887 * jax.random.uniform(keys[8], (VISITS,), jnp.float32) ** block_levels(keys[8], (VISITS,), ((0, 8),), -0.2, 0.2)), 0.25, 4.0),
        "clip_masks": place_ends((jax.random.randint(keys[9], (VISITS, H, W), 0, 8) < 7).astype(jnp.int32), jax.random.fold_in(keys[9], 1), 0, 1),
        "decorrelation": gaussian(keys[10], (VISITS, KS, KS), (KS * KS) ** -0.5, 0.25, ((0, 8),), jnp.float32),
    }


def correlate(pixels, kernel):
    half_width = KS // 2
    result = lax.conv_general_dilated(pixels[None, None], kernel[None, None], (1, 1), ((half_width, half_width), (half_width, half_width)), precision=lax.Precision.HIGHEST)
    return result[0, 0]


def reference(science, basis_kernels, basis_coeffs, row_starts, row_taps, col_offsets, col_starts, col_taps, visit_weights, clip_masks, decorrelation):
    def warp_visit(operands):
        pixels, mixing, shift_rows, taps_rows, dither, shift_cols, taps_cols, weight_now, mask_now = operands
        kernel = jnp.einsum("b,bij->ij", mixing, basis_kernels, precision=lax.Precision.HIGHEST)
        matched = correlate(pixels, kernel)
        padded = jnp.pad(matched, ((TAPS, TAPS), (0, 0)))
        row_index = jnp.arange(H, dtype=jnp.int32) + shift_rows + TAPS
        rowwarp = jnp.zeros((H, W), jnp.float32)
        for tap_index in range(TAPS):
            rowwarp = rowwarp + taps_rows[tap_index][:, None] * jnp.take(padded, row_index + tap_index, axis=0)
        widened = jnp.pad(rowwarp, ((0, 0), (DITHER + 3, 8)))
        actual_start = jnp.arange(W, dtype=jnp.int32) - dither + shift_cols
        warped = jnp.zeros((H, W), jnp.float32)
        for tap_index in range(TAPS):
            warped = warped + taps_cols[tap_index][None, :] * jnp.take(widened, actual_start + DITHER + 3 + tap_index, axis=1)
        covered = ((actual_start >= 0) & (actual_start <= W - TAPS)).astype(jnp.float32)
        share = weight_now * mask_now.astype(jnp.float32) * covered[None, :]
        return warped, share

    warped, share = lax.map(warp_visit, (science, basis_coeffs, row_starts, row_taps, col_offsets, col_starts, col_taps, visit_weights, clip_masks))
    numerator = jnp.sum(share * warped, axis=0)
    denominator = jnp.sum(share, axis=0)
    template = numerator / jnp.maximum(denominator, 1.0)

    def clean_visit(operands):
        warped_now, kernel_now = operands
        return correlate(warped_now - template, kernel_now)

    decorrelated = lax.map(clean_visit, (warped, decorrelation))
    return decorrelated, template
```

```python
import functools

import jax
import jax.numpy as jnp
from jax import lax
from jax.experimental import pallas as pl
from jax.experimental.pallas import tpu as pltpu
from jax.sharding import PartitionSpec as P

KS = 21
HALF = KS // 2
TAPS = 8
PAD = 128
CHUNK = 512
F32 = jnp.float32
BF16 = jnp.bfloat16
MESH = pl.DeviceIdType.MESH
VMEM = pl.BlockSpec(memory_space=pltpu.VMEM)
SMEM = pl.BlockSpec(memory_space=pltpu.SMEM)


def padded_width(columns):
    return -(-(columns + 2 * PAD) // CHUNK) * CHUNK


def split(x):
    high = x.astype(BF16)
    low = (x - high.astype(F32)).astype(BF16)
    return high, low


def toeplitz(kernel_t, c, rows, lead):
    line = jnp.broadcast_to(kernel_t[c : c + 1, :], (rows, 128))
    return pltpu.roll(line, lead, 1, stride=1, stride_axis=0)


def kernel_transposed(kernel, square):
    square[...] = jnp.zeros_like(square)
    square[0:KS, 0:KS] = kernel
    return jnp.transpose(square[...])


def correlate_into(data, hi, lo, partial, emit, rows, depth, group, columns):
    groups = -(-KS // group)
    padded = padded_width(columns)

    @pl.loop(0, padded // CHUNK)
    def _(step):
        start = pl.multiple_of(step * CHUNK, CHUNK)
        window = data[:, pl.ds(start, CHUNK + 128)]
        parts = [window[:, b : b + CHUNK] for b in range(group)]
        parts = [split(part) for part in parts]
        high = jnp.concatenate([part[0] for part in parts], axis=0)
        low = jnp.concatenate([part[1] for part in parts], axis=0)
        total = jnp.dot(hi[...], high, preferred_element_type=F32)
        total = total + jnp.dot(lo[...], high, preferred_element_type=F32)
        total = total + jnp.dot(hi[...], low, preferred_element_type=F32)
        partial[:, pl.ds(start, CHUNK)] = total

    @pl.loop(0, columns // CHUNK)
    def _(step):
        start = pl.multiple_of(step * CHUNK, CHUNK)
        total = jnp.zeros((rows, CHUNK), F32)
        for a in range(groups):
            window = partial[a * rows : (a + 1) * rows, pl.ds(start, CHUNK + 2 * PAD)]
            shift = PAD + group * a - HALF
            total = total + window[:, shift : shift + CHUNK]
        emit(start, total)


def unpack_pair(target, row, packed, columns):
    quarter = columns // 4
    for q in range(4):
        target[row : row + 2, PAD + q * quarter : PAD + (q + 1) * quarter] = packed[2 * q : 2 * q + 2, :]


def pack_pair(packed, source, row, columns):
    quarter = columns // 4
    for q in range(4):
        packed[2 * q : 2 * q + 2, :] = source[row : row + 2, q * quarter : (q + 1) * quarter]


def greet(nv, nr):
    v, r = lax.axis_index("visit"), lax.axis_index("row")
    half = nv // 2
    parity, mine = v % 2, v // 2
    barrier = pltpu.get_barrier_semaphore()

    def hello(a, b):
        pl.semaphore_signal(barrier, inc=1, device_id=(a, b), device_id_type=MESH)

    hello(v + 1 - 2 * parity, r)
    for d in range(1, half):
        hello(2 * ((mine + d) % half) + parity, r)

    @pl.when(r > 0)
    def _():
        hello(v, r - 1)

    @pl.when(r < nr - 1)
    def _():
        hello(v, r + 1)

    above, below = (r > 0).astype(jnp.int32), (r < nr - 1).astype(jnp.int32)
    pl.semaphore_wait(barrier, half + above + below)


def remote(src, dst, send, recv, device):
    return pltpu.make_async_remote_copy(
        src_ref=src, dst_ref=dst, send_sem=send, recv_sem=recv, device_id=device, device_id_type=MESH
    )


def pair_start(nv, blocks, landed, sems):
    v, r = lax.axis_index("visit"), lax.axis_index("row")
    half = nv // 2
    parity, mine = v % 2, v // 2
    copies = {}
    for d in list(range(1, half)) + [0]:
        k = (mine + d) % half
        copies[d] = remote(
            blocks.at[2 * k + 1 - parity], landed.at[k], sems.at[0, d], sems.at[1, d], (v + 1 - 2 * parity, r)
        )
        copies[d].start()
    return copies


def scatter_sum(nv, blocks, landed, pair_copies, sums, arrived, sems):
    v, r = lax.axis_index("visit"), lax.axis_index("row")
    half = nv // 2
    parity, mine = v % 2, v // 2
    copies = []
    for d in range(1, half):
        k = (mine + d) % half
        pair_copies[d].wait()
        sums[d - 1] = blocks[2 * k + parity] + landed[k]
        copy = remote(sums.at[d - 1], arrived.at[d - 1], sems.at[0, d], sems.at[1, d], (2 * k + parity, r))
        copy.start()
        copies.append(copy)
    pair_copies[0].wait()
    total = blocks[v] + landed[mine]
    for d in range(1, half):
        copies[d - 1].wait()
        total = total + arrived[d - 1]
    return total


def sum_scratch(nv, rows, width):
    half = nv // 2
    return [
        pltpu.VMEM((half, rows, width), F32),
        pltpu.VMEM((half - 1, rows, width), F32),
        pltpu.VMEM((half - 1, rows, width), F32),
        pltpu.SemaphoreType.DMA((2, half)),
        pltpu.SemaphoreType.DMA((2, half)),
    ]


def first_kernel(
    nv, nr, science, masks, col_starts, offsets, weights,
    top, top_pair, bottom, bottom_pair, denominator,
    pack_top, pack_bottom, blocks, landed, sums, arrived, pair_sems, sum_sems, halo_sems,
):
    v, r = lax.axis_index("visit"), lax.axis_index("row")
    rows, columns = science.shape
    width = columns // nv
    pack_pair(pack_top, science, 16, columns)
    pack_pair(pack_bottom, science, rows - 18, columns)
    greet(nv, nr)
    up = [
        remote(science.at[0:16], bottom, halo_sems.at[0, 0], halo_sems.at[1, 0], (v, r - 1)),
        remote(pack_top, bottom_pair, halo_sems.at[0, 1], halo_sems.at[1, 1], (v, r - 1)),
    ]
    down = [
        remote(science.at[rows - 16 : rows], top, halo_sems.at[0, 2], halo_sems.at[1, 2], (v, r + 1)),
        remote(pack_bottom, top_pair, halo_sems.at[0, 3], halo_sems.at[1, 3], (v, r + 1)),
    ]

    @pl.when(r > 0)
    def _():
        for copy in up:
            copy.start()

    @pl.when(r < nr - 1)
    def _():
        for copy in down:
            copy.start()

    @pl.when(r == 0)
    def _():
        top[...] = jnp.zeros_like(top)
        top_pair[...] = jnp.zeros_like(top_pair)

    @pl.when(r == nr - 1)
    def _():
        bottom[...] = jnp.zeros_like(bottom)
        bottom_pair[...] = jnp.zeros_like(bottom_pair)

    for u in range(nv):
        span = slice(u * width, (u + 1) * width)
        start = col_starts[:, span] + (
            lax.broadcasted_iota(jnp.int32, (1, width), 1) + (u * width - offsets[0])
        )
        covered = jnp.where((start >= 0) & (start <= columns - TAPS), weights[0], 0.0)
        blocks[u] = masks[:, span].astype(F32) * covered
    pair_copies = pair_start(nv, blocks, landed, pair_sems)
    denominator[...] = scatter_sum(nv, blocks, landed, pair_copies, sums, arrived, sum_sems)

    @pl.when(r > 0)
    def _():
        for copy in up:
            copy.wait_send()
        for copy in down:
            copy.wait_recv()

    @pl.when(r < nr - 1)
    def _():
        for copy in down:
            copy.wait_send()
        for copy in up:
            copy.wait_recv()


def match_kernel(
    science, top, top_pair, bottom, bottom_pair, basis, coeffs, row_starts, row_taps, edges,
    offsets, col_starts, col_taps, weights, masks,
    warped, numerator,
    data, square, flat, hi, lo, partial, shifted,
):
    rows, columns = science.shape
    nv, _, width = numerator.shape
    depth, group = 80, 3
    middle = rows + 2 * TAPS
    data[...] = jnp.zeros_like(data)
    data[8:24, PAD : PAD + columns] = top[...]
    data[24 : 24 + rows, PAD : PAD + columns] = science[...]
    data[24 + rows : 40 + rows, PAD : PAD + columns] = bottom[...]
    unpack_pair(data, 6, top_pair, columns)
    unpack_pair(data, 40 + rows, bottom_pair, columns)
    kernel = coeffs[0] * basis[0]
    for b in range(1, basis.shape[0]):
        kernel = kernel + coeffs[b] * basis[b]
    kernel_t = kernel_transposed(kernel, square)
    m = lax.broadcasted_iota(jnp.int32, (middle, rows), 0) - TAPS
    i = lax.broadcasted_iota(jnp.int32, (middle, rows), 1)
    tap = m - i - row_starts[...]
    inside = (m + edges[0] >= 0) & (m + edges[0] < edges[1])
    mix = jnp.zeros((middle, rows), F32)
    for t in range(TAPS):
        mix = mix + jnp.where((tap == t) & inside, row_taps[t : t + 1, :], 0.0)
    flat[...] = jnp.zeros_like(flat)
    for c in range(KS):
        band = toeplitz(kernel_t, c, middle, 6)
        folded = lax.dot_general(
            mix, band, (((0,), (0,)), ((), ())), precision=lax.Precision.HIGHEST, preferred_element_type=F32
        )
        a, b = c // group, c % group
        flat[a * rows : (a + 1) * rows, b * depth : (b + 1) * depth] = folded[:, :depth]
    high, low = split(flat[...])
    hi[...] = high
    lo[...] = low
    dither = offsets[0]
    tiles = dither // 128
    within = dither % 128
    shifted[...] = jnp.zeros_like(shifted)

    def keep(start, values):
        shifted[:, pl.ds(pl.multiple_of(start + 640, 128), CHUNK)] = values

    correlate_into(data, hi, lo, partial, keep, rows, depth, group, columns)

    @pl.loop(0, nv)
    def _(u):
        start = pl.multiple_of(u * width, width)
        base = pl.multiple_of(start + 384 - tiles * 128, 128)
        window = shifted[:, pl.ds(base, width + 384)]
        window = pltpu.roll(window, within, 1)
        early = col_starts[:, pl.ds(start, width)] == -3
        taps = [col_taps[t : t + 1, pl.ds(start, width)] for t in range(TAPS)]
        total = jnp.zeros((rows, width), F32)
        for lag in range(TAPS + 1):
            now = taps[lag] if lag < TAPS else jnp.zeros_like(taps[0])
            before = taps[lag - 1] if lag > 0 else jnp.zeros_like(taps[0])
            at = 256 + lag - 3
            total = total + jnp.where(early, now, before) * window[:, at : at + width]
        warped[:, pl.ds(start, width)] = total
        first = col_starts[:, pl.ds(start, width)] + (
            lax.broadcasted_iota(jnp.int32, (1, width), 1) + (start - dither)
        )
        covered = jnp.where((first >= 0) & (first <= columns - TAPS), weights[0], 0.0)
        numerator[u] = masks[:, pl.ds(start, width)].astype(F32) * covered * total


def coadd_kernel(
    nv, nr, numerator, denominator, warped,
    template, difference, top, top_pair, bottom, bottom_pair,
    pack_top, pack_bottom, gathered, landed, sums, arrived, pair_sems, sum_sems, gather_sems, pass_sems, halo_sems,
):
    v, r = lax.axis_index("visit"), lax.axis_index("row")
    half = nv // 2
    parity, mine = v % 2, v // 2
    partner = (v + 1 - 2 * parity, r)
    rows, columns = warped.shape
    width = columns // nv
    greet(nv, nr)
    pair_copies = pair_start(nv, numerator, landed, pair_sems)

    @pl.when(r == 0)
    def _():
        top[...] = jnp.zeros_like(top)
        top_pair[...] = jnp.zeros_like(top_pair)

    @pl.when(r == nr - 1)
    def _():
        bottom[...] = jnp.zeros_like(bottom)
        bottom_pair[...] = jnp.zeros_like(bottom_pair)

    total = scatter_sum(nv, numerator, landed, pair_copies, sums, arrived, sum_sems)
    own = total / jnp.maximum(denominator[...], 1.0)
    template[...] = own
    gathered[v] = own
    sends = []
    for d in range(1, half):
        k = (mine + d) % half
        copy = remote(gathered.at[v], gathered.at[v], gather_sems.at[0, d], gather_sems.at[1, d], (2 * k + parity, r))
        copy.start()
        sends.append(copy)

    def passed(d):
        k = (mine + half - d) % half
        u = 2 * k + parity
        return remote(gathered.at[u], gathered.at[u], pass_sems.at[0, d], pass_sems.at[1, d], partner)

    passes = [passed(d) for d in range(half)]
    passes[0].start()

    def halo(u, index, up):
        span = pl.ds(pl.multiple_of(u * width, width), width)
        if up:
            return remote(
                difference.at[0:8, span], bottom.at[:, span],
                halo_sems.at[0, index], halo_sems.at[1, index], (v, r - 1),
            )
        return remote(
            difference.at[rows - 8 : rows, span], top.at[:, span],
            halo_sems.at[2, index], halo_sems.at[3, index], (v, r + 1),
        )

    ups, downs = [], []

    def subtract(u):
        span = pl.ds(pl.multiple_of(u * width, width), width)
        difference[:, span] = warped[:, span] - gathered[u]
        ups.append(halo(u, len(ups), True))
        downs.append(halo(u, len(downs), False))

        @pl.when(r > 0)
        def _():
            ups[-1].start()

        @pl.when(r < nr - 1)
        def _():
            downs[-1].start()

    subtract(v)
    for d in range(half):
        if d > 0:
            sends[d - 1].wait_recv()
            passes[d].start()
            subtract(2 * ((mine + half - d) % half) + parity)
        passes[d].wait_recv()
        subtract(2 * ((mine + half - d) % half) + 1 - parity)
    pack_pair(pack_top, difference, 8, columns)
    pack_pair(pack_bottom, difference, rows - 10, columns)
    ups.append(remote(pack_top, bottom_pair, halo_sems.at[0, nv], halo_sems.at[1, nv], (v, r - 1)))
    downs.append(remote(pack_bottom, top_pair, halo_sems.at[2, nv], halo_sems.at[3, nv], (v, r + 1)))

    @pl.when(r > 0)
    def _():
        ups[-1].start()

    @pl.when(r < nr - 1)
    def _():
        downs[-1].start()

    for copy in sends + passes:
        copy.wait_send()

    @pl.when(r > 0)
    def _():
        for copy in ups:
            copy.wait_send()
        for copy in downs:
            copy.wait_recv()

    @pl.when(r < nr - 1)
    def _():
        for copy in downs:
            copy.wait_send()
        for copy in ups:
            copy.wait_recv()


def clean_kernel(
    difference, top, top_pair, bottom, bottom_pair, decorrelation, cleaned, data, square, flat, hi, lo, partial
):
    rows, columns = difference.shape
    depth, group = 64, 4
    data[...] = jnp.zeros_like(data)
    data[8:16, PAD : PAD + columns] = top[...]
    data[16 : 16 + rows, PAD : PAD + columns] = difference[...]
    data[16 + rows : 24 + rows, PAD : PAD + columns] = bottom[...]
    unpack_pair(data, 6, top_pair, columns)
    unpack_pair(data, 24 + rows, bottom_pair, columns)
    kernel_t = kernel_transposed(decorrelation[...], square)
    flat[...] = jnp.zeros_like(flat)
    for c in range(KS):
        band = toeplitz(kernel_t, c, rows, 6)
        a, b = c // group, c % group
        flat[a * rows : (a + 1) * rows, b * depth : (b + 1) * depth] = band[:, :depth]
    high, low = split(flat[...])
    hi[...] = high
    lo[...] = low

    def keep(start, values):
        cleaned[:, pl.ds(start, CHUNK)] = values

    correlate_into(data, hi, lo, partial, keep, rows, depth, group, columns)


def correlate_scratch(rows, depth, group, columns):
    groups = -(-KS // group)
    padded = padded_width(columns)
    return [
        pltpu.VMEM((depth, padded + 128), F32),
        pltpu.VMEM((128, 128), F32),
        pltpu.VMEM((groups * rows, group * depth), F32),
        pltpu.VMEM((groups * rows, group * depth), BF16),
        pltpu.VMEM((groups * rows, group * depth), BF16),
        pltpu.VMEM((groups * rows, padded), F32),
    ]


def shape(*dims):
    return jax.ShapeDtypeStruct(dims, F32)


def on_device(
    nv, nr, science, basis_kernels, basis_coeffs, row_starts, row_taps, col_offsets,
    col_starts, col_taps, visit_weights, clip_masks, decorrelation,
):
    pixels = science[0]
    masks = clip_masks[0]
    rows, columns = pixels.shape
    width = columns // nv
    limit = 60 * 1024 * 1024
    remote_params = lambda cid: pltpu.CompilerParams(
        collective_id=cid, has_side_effects=True, vmem_limit_bytes=limit
    )
    top, top_pair, bottom, bottom_pair, denominator = pl.pallas_call(
        functools.partial(first_kernel, nv, nr),
        out_shape=(
            shape(16, columns), shape(8, columns // 4), shape(16, columns), shape(8, columns // 4), shape(rows, width)
        ),
        in_specs=[VMEM, VMEM, VMEM, SMEM, SMEM],
        out_specs=(VMEM,) * 5,
        scratch_shapes=[
            pltpu.VMEM((8, columns // 4), F32),
            pltpu.VMEM((8, columns // 4), F32),
            pltpu.VMEM((nv, rows, width), F32),
        ] + sum_scratch(nv, rows, width) + [pltpu.SemaphoreType.DMA((2, 4))],
        compiler_params=remote_params(0),
        name="halo",
    )(pixels, masks, col_starts, col_offsets, visit_weights)
    first_row = lax.axis_index("row") * rows
    edges = jnp.stack([first_row, jnp.int32(rows * nr)])
    warped, numerator = pl.pallas_call(
        match_kernel,
        out_shape=(shape(rows, columns), shape(nv, rows, width)),
        in_specs=[VMEM] * 6 + [SMEM, VMEM, VMEM, SMEM, SMEM, VMEM, VMEM, SMEM, VMEM],
        out_specs=(VMEM, VMEM),
        scratch_shapes=correlate_scratch(rows, 80, 3, columns) + [pltpu.VMEM((rows, columns + 1024), F32)],
        compiler_params=pltpu.CompilerParams(vmem_limit_bytes=limit),
        name="match",
    )(
        pixels, top, top_pair, bottom, bottom_pair, basis_kernels, basis_coeffs[0], row_starts, row_taps[0], edges,
        col_offsets, col_starts, col_taps[0], visit_weights, masks,
    )
    template, difference, top, top_pair, bottom, bottom_pair = pl.pallas_call(
        functools.partial(coadd_kernel, nv, nr),
        out_shape=(
            shape(rows, width), shape(rows, columns),
            shape(8, columns), shape(8, columns // 4), shape(8, columns), shape(8, columns // 4),
        ),
        in_specs=[VMEM] * 3,
        out_specs=(VMEM,) * 6,
        scratch_shapes=[
            pltpu.VMEM((8, columns // 4), F32),
            pltpu.VMEM((8, columns // 4), F32),
            pltpu.VMEM((nv, rows, width), F32),
        ] + sum_scratch(nv, rows, width) + [
            pltpu.SemaphoreType.DMA((2, nv // 2)),
            pltpu.SemaphoreType.DMA((2, nv // 2)),
            pltpu.SemaphoreType.DMA((4, nv + 1)),
        ],
        compiler_params=remote_params(1),
        name="coadd",
    )(numerator, denominator, warped)
    cleaned = pl.pallas_call(
        clean_kernel,
        out_shape=shape(rows, columns),
        in_specs=[VMEM] * 6,
        out_specs=VMEM,
        scratch_shapes=correlate_scratch(rows, 64, 4, columns),
        compiler_params=pltpu.CompilerParams(vmem_limit_bytes=limit),
        name="clean",
    )(difference, top, top_pair, bottom, bottom_pair, decorrelation[0])
    return (cleaned[None], template)


def solution(mesh):
    nv, nr = mesh.shape["visit"], mesh.shape["row"]
    return jax.shard_map(
        functools.partial(on_device, nv, nr),
        mesh=mesh,
        in_specs=(
            P("visit", "row", None),
            P(),
            P("visit", None),
            P("visit", "row"),
            P("visit", None, "row"),
            P("visit"),
            P("visit", None),
            P("visit", None, None),
            P("visit"),
            P("visit", "row", None),
            P("visit", None, None),
        ),
        out_specs=(P("visit", "row", None), P("row", "visit")),
        check_vma=False,
    )
```

```python
import functools

import jax
import jax.numpy as jnp
from jax import lax
from jax.experimental import pallas as pl
from jax.experimental.pallas import tpu as pltpu
from jax.sharding import PartitionSpec as P

KS = 21
HALF = KS // 2
TAPS = 8
PAD = 128
CHUNK = 512
F32 = jnp.float32
BF16 = jnp.bfloat16
MESH = pl.DeviceIdType.MESH
VMEM = pl.BlockSpec(memory_space=pltpu.VMEM)
SMEM = pl.BlockSpec(memory_space=pltpu.SMEM)


def padded_width(columns):
    return -(-(columns + 2 * PAD) // CHUNK) * CHUNK


def split(x):
    high = x.astype(BF16)
    low = (x - high.astype(F32)).astype(BF16)
    return high, low


def toeplitz(kernel_t, c, rows, lead):
    line = jnp.broadcast_to(kernel_t[c : c + 1, :], (rows, 128))
    return pltpu.roll(line, lead, 1, stride=1, stride_axis=0)


def kernel_transposed(kernel, square):
    square[...] = jnp.zeros_like(square)
    square[0:KS, 0:KS] = kernel
    return jnp.transpose(square[...])


def piece(high, low, hi, lo, partial, start, group, add=False):
    m = hi.shape[0]
    window_h = high[:, start : start + CHUNK + 128]
    window_l = low[:, start : start + CHUNK + 128]
    stack_h = jnp.concatenate([window_h[:, b : b + CHUNK] for b in range(group)], axis=0)
    stack_l = jnp.concatenate([window_l[:, b : b + CHUNK] for b in range(group)], axis=0)
    total = jnp.dot(hi[...], stack_h, preferred_element_type=F32)
    total = total + jnp.dot(lo[...], stack_h, preferred_element_type=F32)
    total = total + jnp.dot(hi[...], stack_l, preferred_element_type=F32)
    if add:
        total = total + partial[0:m, start : start + CHUNK]
    partial[0:m, start : start + CHUNK] = total


def shifted_sum(partial, start, rows, group):
    total = jnp.zeros((rows, CHUNK), F32)
    for a in range(-(-KS // group)):
        window = partial[a * rows : (a + 1) * rows, start : start + CHUNK + 2 * PAD]
        shift = PAD + group * a - HALF
        total = total + window[:, shift : shift + CHUNK]
    return total


def store_split(high, low, row, column, values):
    h, l = split(values)
    high[row : row + values.shape[0], column : column + values.shape[1]] = h
    low[row : row + values.shape[0], column : column + values.shape[1]] = l


def pack_pair(packed, source, row, columns):
    quarter = columns // 4
    for q in range(4):
        packed[2 * q : 2 * q + 2, :] = source[row : row + 2, q * quarter : (q + 1) * quarter]


def greet(nv, nr):
    v, r = lax.axis_index("visit"), lax.axis_index("row")
    half = nv // 2
    parity, mine = v % 2, v // 2
    barrier = pltpu.get_barrier_semaphore()

    def hello(a, b):
        pl.semaphore_signal(barrier, inc=1, device_id=(a, b), device_id_type=MESH)

    hello(v + 1 - 2 * parity, r)
    for d in range(1, half):
        hello(2 * ((mine + d) % half) + parity, r)

    @pl.when(r > 0)
    def _():
        hello(v, r - 1)

    @pl.when(r < nr - 1)
    def _():
        hello(v, r + 1)

    above, below = (r > 0).astype(jnp.int32), (r < nr - 1).astype(jnp.int32)
    pl.semaphore_wait(barrier, half + above + below)


def remote(src, dst, send, recv, device):
    return pltpu.make_async_remote_copy(
        src_ref=src, dst_ref=dst, send_sem=send, recv_sem=recv, device_id=device, device_id_type=MESH
    )


def pair_start(nv, blocks, landed, sems):
    v, r = lax.axis_index("visit"), lax.axis_index("row")
    half = nv // 2
    parity, mine = v % 2, v // 2
    copies = {}
    for d in list(range(1, half)) + [0]:
        k = (mine + d) % half
        copies[d] = remote(
            blocks.at[2 * k + 1 - parity], landed.at[k], sems.at[0, d], sems.at[1, d], (v + 1 - 2 * parity, r)
        )
        copies[d].start()
    return copies


def scatter_sum(nv, blocks, landed, pair_copies, sums, arrived, sems):
    v, r = lax.axis_index("visit"), lax.axis_index("row")
    half = nv // 2
    parity, mine = v % 2, v // 2
    copies = []
    for d in range(1, half):
        k = (mine + d) % half
        pair_copies[d].wait()
        sums[d - 1] = blocks[2 * k + parity] + landed[k]
        copy = remote(sums.at[d - 1], arrived.at[d - 1], sems.at[0, d], sems.at[1, d], (2 * k + parity, r))
        copy.start()
        copies.append(copy)
    pair_copies[0].wait()
    total = blocks[v] + landed[mine]
    for d in range(1, half):
        copies[d - 1].wait()
        total = total + arrived[d - 1]
    return total


def exchange_scratch(nv, rows, width):
    half = nv // 2
    return [
        pltpu.VMEM((half, rows, width), F32),
        pltpu.VMEM((half, rows, width), F32),
        pltpu.VMEM((half, rows, width), F32),
        pltpu.SemaphoreType.DMA((2, half)),
        pltpu.SemaphoreType.DMA((2, half)),
    ]


def whole_kernel(
    nv, nr, science, basis, coeffs, row_starts, row_taps, offsets, col_starts, col_taps, weights, masks, decor,
    cleaned, template,
    shares, numerators, warped, difference, gathered, denominator,
    near_top, near_bottom, packs, pairs_top, pairs_bottom,
    late_top, late_bottom, late_pack_top, late_pack_bottom, late_pair_top, late_pair_bottom,
    square, bands, flat, hi, lo, flat_own, own_hi, own_lo, flat_edge, edge_hi, edge_lo,
    high, low, second_high, second_low, edge_high, edge_low, partial, shifted, mover,
    d_landed, d_sums, d_arrived, d_pair, d_sum,
    n_landed, n_sums, n_arrived, n_pair, n_sum,
    gather_sems, pass_sems, halo_sems, late_sems,
):
    v, r = lax.axis_index("visit"), lax.axis_index("row")
    rows, columns = science.shape
    width = columns // nv
    half = nv // 2
    parity, mine = v % 2, v // 2
    partner = (v + 1 - 2 * parity, r)
    chunks = packs.shape[1]
    span = columns // chunks
    padded = padded_width(columns)
    depth, group = high.shape[0], 3
    middle = rows + 2 * TAPS

    quarter = span // 4
    for n in range(chunks):
        for q in range(4):
            at = n * span + q * quarter
            packs[0, n, 2 * q : 2 * q + 2, :] = science[16:18, at : at + quarter]
            packs[1, n, 2 * q : 2 * q + 2, :] = science[rows - 18 : rows - 16, at : at + quarter]
    greet(nv, nr)
    up, down = [], []
    for n in range(chunks):
        cols = slice(n * span, (n + 1) * span)
        up.append(remote(science.at[0:16, cols], near_bottom.at[:, cols], halo_sems.at[0, n], halo_sems.at[1, n], (v, r - 1)))
        up.append(remote(packs.at[0, n], pairs_bottom.at[n], halo_sems.at[2, n], halo_sems.at[3, n], (v, r - 1)))
        down.append(remote(science.at[rows - 16 : rows, cols], near_top.at[:, cols], halo_sems.at[4, n], halo_sems.at[5, n], (v, r + 1)))
        down.append(remote(packs.at[1, n], pairs_top.at[n], halo_sems.at[6, n], halo_sems.at[7, n], (v, r + 1)))

    @pl.when(r > 0)
    def _():
        for copy in up:
            copy.start()

    @pl.when(r < nr - 1)
    def _():
        for copy in down:
            copy.start()

    @pl.when(r == 0)
    def _():
        near_top[...] = jnp.zeros_like(near_top)
        pairs_top[...] = jnp.zeros_like(pairs_top)
        late_top[...] = jnp.zeros_like(late_top)
        late_pair_top[...] = jnp.zeros_like(late_pair_top)

    @pl.when(r == nr - 1)
    def _():
        near_bottom[...] = jnp.zeros_like(near_bottom)
        pairs_bottom[...] = jnp.zeros_like(pairs_bottom)
        late_bottom[...] = jnp.zeros_like(late_bottom)
        late_pair_bottom[...] = jnp.zeros_like(late_pair_bottom)

    dither = offsets[0]
    for u in range(nv):
        cols = slice(u * width, (u + 1) * width)
        start = col_starts[:, cols] + (lax.broadcasted_iota(jnp.int32, (1, width), 1) + (u * width - dither))
        covered = jnp.where((start >= 0) & (start <= columns - TAPS), weights[0], 0.0)
        shares[u] = masks[:, cols].astype(F32) * covered
    weight_pairs = pair_start(nv, shares, d_landed, d_pair)

    kernel = coeffs[0] * basis[0]
    for b in range(1, basis.shape[0]):
        kernel = kernel + coeffs[b] * basis[b]
    kernel_t = kernel_transposed(kernel, square)
    m = lax.broadcasted_iota(jnp.int32, (middle, rows), 0) - TAPS
    i = lax.broadcasted_iota(jnp.int32, (middle, rows), 1)
    tap = m - i - row_starts[...]
    inside = (m + r * rows >= 0) & (m + r * rows < nr * rows)
    mix = jnp.zeros((middle, rows), F32)
    for t in range(TAPS):
        mix = mix + jnp.where((tap == t) & inside, row_taps[t : t + 1, :], 0.0)
    for c in range(KS):
        bands[:, c * 128 : (c + 1) * 128] = toeplitz(kernel_t, c, middle, 6)
    folded = lax.dot_general(
        mix, bands[...], (((0,), (0,)), ((), ())), precision=lax.Precision.HIGHEST, preferred_element_type=F32
    )
    flat[...] = jnp.zeros_like(flat)
    for c in range(KS):
        a, b = c // group, c % group
        flat[a * rows : (a + 1) * rows, b * depth : (b + 1) * depth] = folded[:, c * 128 : c * 128 + depth]
    h, l = split(flat[...])
    hi[...] = h
    lo[...] = l

    kernel_t = kernel_transposed(decor[:, 0, :], square)
    flat_own[...] = jnp.zeros_like(flat_own)
    flat_edge[...] = jnp.zeros_like(flat_edge)
    for c in range(KS):
        band = toeplitz(kernel_t, c, rows, 6)
        a, b = c // 8, c % 8
        here = slice(a * rows, (a + 1) * rows)
        flat_own[here, b * rows : (b + 1) * rows] = band[:, 16 : 16 + rows]
        flat_edge[here, b * 32 : b * 32 + 16] = band[:, 0:16]
        flat_edge[here, b * 32 + 16 : b * 32 + 32] = band[:, 16 + rows : 32 + rows]
    h, l = split(flat_own[...])
    own_hi[...] = h
    own_lo[...] = l
    h, l = split(flat_edge[...])
    edge_hi[...] = h
    edge_lo[...] = l

    for frame in (high, low, second_high, second_low, edge_high, edge_low):
        frame[...] = jnp.zeros_like(frame)
    shifted[...] = jnp.zeros_like(shifted)
    denominator[...] = scatter_sum(nv, shares, d_landed, weight_pairs, d_sums, d_arrived, d_sum)

    tiles = jnp.full((rows, width + 384), dither // 128, jnp.int32)
    place = lax.broadcasted_iota(jnp.int32, (256, 128), 0) - lax.broadcasted_iota(jnp.int32, (256, 128), 1)
    mover[...] = jnp.where(place == 128 - dither % 128, 1.0, 0.0).astype(BF16)

    def warp(u):
        start = u * width
        count = width // 128 + 2
        window = shifted[:, start + 384 : start + 768 + width]
        for t in range(1, 4):
            at = start + 384 - 128 * t
            window = jnp.where(tiles == t, shifted[:, at : at + width + 384], window)
        h, l = split(window)
        stack_h = jnp.concatenate([h[:, 128 * j : 128 * j + 256] for j in range(count)], axis=0)
        stack_l = jnp.concatenate([l[:, 128 * j : 128 * j + 256] for j in range(count)], axis=0)
        moved = jnp.dot(stack_h, mover[...], preferred_element_type=F32)
        moved = moved + jnp.dot(stack_l, mover[...], preferred_element_type=F32)
        window = jnp.concatenate([moved[j * rows : (j + 1) * rows] for j in range(count)], axis=1)
        cols = slice(start, start + width)
        early = col_starts[:, cols] == -3
        taps = [col_taps[t : t + 1, cols] for t in range(TAPS)]
        total = jnp.zeros((rows, width), F32)
        for lag in range(TAPS + 1):
            now = taps[lag] if lag < TAPS else jnp.zeros_like(taps[0])
            before = taps[lag - 1] if lag > 0 else jnp.zeros_like(taps[0])
            at = 128 + lag - 3
            total = total + jnp.where(early, now, before) * window[:, at : at + width]
        warped[:, cols] = total
        numerators[u] = shares[u] * total

    def number_pair(k):
        return remote(numerators.at[2 * k + 1 - parity], n_landed.at[k], n_pair.at[0, k], n_pair.at[1, k], partner)

    def number_sum(k, d):
        return remote(n_sums.at[k], n_arrived.at[d], n_sum.at[0, d], n_sum.at[1, d], (2 * k + parity, r))

    def forward(k):
        number_pair(k).wait()
        n_sums[k] = numerators[2 * k + parity] + n_landed[k]
        d = (k - mine + half) % half

        @pl.when(d > 0)
        def _():
            number_sum(k, d).start()

    pieces = padded // CHUNK
    done_pieces, done_sums, done_warps, done_pairs, done_forwards = 0, 0, 0, 0, 0
    for n in range(chunks):
        cols = slice(n * span, (n + 1) * span)

        @pl.when(r > 0)
        def _():
            down[2 * n].wait_recv()
            down[2 * n + 1].wait_recv()

        @pl.when(r < nr - 1)
        def _():
            up[2 * n].wait_recv()
            up[2 * n + 1].wait_recv()

        store_split(high, low, 24, PAD + n * span, science[:, cols])
        top = near_top[:, cols]
        bottom = near_bottom[:, cols]
        store_split(high, low, 8, PAD + n * span, top)
        store_split(high, low, 24 + rows, PAD + n * span, bottom)
        for q in range(4):
            at = PAD + n * span + q * quarter
            store_split(high, low, 6, at, pairs_top[n, 2 * q : 2 * q + 2, :])
            store_split(high, low, 40 + rows, at, pairs_bottom[n, 2 * q : 2 * q + 2, :])
        last = n == chunks - 1
        while done_pieces < pieces and (last or (done_pieces + 1) * CHUNK + group - PAD <= (n + 1) * span):
            piece(high, low, hi, lo, partial, done_pieces * CHUNK, group)
            done_pieces += 1
        while done_sums < columns // CHUNK and done_sums + 2 <= done_pieces:
            start = done_sums * CHUNK
            shifted[:, 640 + start : 640 + start + CHUNK] = shifted_sum(partial, start, rows, group)
            done_sums += 1
        while done_warps < nv and (done_sums * CHUNK >= (done_warps + 1) * width + 8 or done_sums * CHUNK == columns):
            warp(done_warps)
            done_warps += 1
            if done_warps % 2 == 0:
                number_pair(done_pairs).start()
                done_pairs += 1
                if done_pairs >= 2:
                    forward(done_forwards)
                    done_forwards += 1
    while done_forwards < half:
        forward(done_forwards)
        done_forwards += 1

    total = n_sums[mine]
    for d in range(1, half):
        number_sum((mine + d) % half, d).wait()
        total = total + n_arrived[d]
    own = total / jnp.maximum(denominator[...], 1.0)
    template[...] = own
    gathered[v] = own
    sends = []
    for d in range(1, half):
        k = (mine + d) % half
        copy = remote(gathered.at[v], gathered.at[v], gather_sems.at[0, d], gather_sems.at[1, d], (2 * k + parity, r))
        copy.start()
        sends.append(copy)

    def passed(d):
        u = 2 * ((mine + half - d) % half) + parity
        return remote(gathered.at[u], gathered.at[u], pass_sems.at[0, d], pass_sems.at[1, d], partner)

    passes = [passed(d) for d in range(half)]
    passes[0].start()
    ups, downs = [], []

    def subtract(u):
        cols = pl.ds(pl.multiple_of(u * width, width), width)
        at = pl.ds(pl.multiple_of(PAD + u * width, 128), width)
        values = warped[:, cols] - gathered[u]
        difference[:, cols] = values
        h, l = split(values)
        second_high[:, at] = h
        second_low[:, at] = l
        n = len(ups)
        ups.append(remote(difference.at[0:8, cols], late_bottom.at[:, cols], late_sems.at[0, n], late_sems.at[1, n], (v, r - 1)))
        downs.append(
            remote(difference.at[rows - 8 : rows, cols], late_top.at[:, cols], late_sems.at[2, n], late_sems.at[3, n], (v, r + 1))
        )

        @pl.when(r > 0)
        def _():
            ups[-1].start()

        @pl.when(r < nr - 1)
        def _():
            downs[-1].start()

    subtract(v)
    for d in range(half):
        if d > 0:
            sends[d - 1].wait_recv()
            passes[d].start()
            subtract(2 * ((mine + half - d) % half) + parity)
        passes[d].wait_recv()
        subtract(2 * ((mine + half - d) % half) + 1 - parity)
    pack_pair(late_pack_top, difference, 8, columns)
    pack_pair(late_pack_bottom, difference, rows - 10, columns)
    ups.append(remote(late_pack_top, late_pair_bottom, late_sems.at[0, nv], late_sems.at[1, nv], (v, r - 1)))
    downs.append(remote(late_pack_bottom, late_pair_top, late_sems.at[2, nv], late_sems.at[3, nv], (v, r + 1)))

    @pl.when(r > 0)
    def _():
        ups[-1].start()

    @pl.when(r < nr - 1)
    def _():
        downs[-1].start()

    for n in range(pieces):
        piece(second_high, second_low, own_hi, own_lo, partial, n * CHUNK, 8)

    @pl.when(r > 0)
    def _():
        for copy in downs:
            copy.wait_recv()

    @pl.when(r < nr - 1)
    def _():
        for copy in ups:
            copy.wait_recv()

    store_split(edge_high, edge_low, 8, PAD, late_top[...])
    store_split(edge_high, edge_low, 16, PAD, late_bottom[...])
    for q in range(4):
        at = PAD + q * (columns // 4)
        store_split(edge_high, edge_low, 6, at, late_pair_top[2 * q : 2 * q + 2, :])
        store_split(edge_high, edge_low, 24, at, late_pair_bottom[2 * q : 2 * q + 2, :])
    for n in range(pieces):
        piece(edge_high, edge_low, edge_hi, edge_lo, partial, n * CHUNK, 8, add=True)
        if n > 0 and n * CHUNK <= columns:
            cleaned[:, (n - 1) * CHUNK : n * CHUNK] = shifted_sum(partial, (n - 1) * CHUNK, rows, 8)

    for copy in sends + passes:
        copy.wait_send()

    @pl.when(r > 0)
    def _():
        for copy in up + ups:
            copy.wait_send()

    @pl.when(r < nr - 1)
    def _():
        for copy in down + downs:
            copy.wait_send()


def shape(*dims):
    return jax.ShapeDtypeStruct(dims, F32)


def on_device(
    nv, nr, science, basis_kernels, basis_coeffs, row_starts, row_taps, col_offsets,
    col_starts, col_taps, visit_weights, clip_masks, decorrelation,
):
    pixels = science[0]
    rows, columns = pixels.shape
    width = columns // nv
    half = nv // 2
    chunks = 4
    span = columns // chunks
    padded = padded_width(columns)
    depth, group = 80, 3
    tall = -(-KS // group) * rows
    wide = -(-KS // 8) * rows
    f32 = lambda *dims: pltpu.VMEM(dims, F32)
    bf16 = lambda *dims: pltpu.VMEM(dims, BF16)
    cleaned, template = pl.pallas_call(
        functools.partial(whole_kernel, nv, nr),
        out_shape=(shape(rows, columns), shape(rows, width)),
        in_specs=[VMEM, VMEM, SMEM, VMEM, VMEM, SMEM, VMEM, VMEM, SMEM, VMEM, VMEM],
        out_specs=(VMEM, VMEM),
        scratch_shapes=[
            f32(nv, rows, width), f32(nv, rows, width), f32(rows, columns), f32(rows, columns),
            f32(nv, rows, width), f32(rows, width),
            f32(16, columns), f32(16, columns), f32(2, chunks, 8, span // 4),
            f32(chunks, 8, span // 4), f32(chunks, 8, span // 4),
            f32(8, columns), f32(8, columns), f32(8, columns // 4), f32(8, columns // 4),
            f32(8, columns // 4), f32(8, columns // 4),
            f32(128, 128), f32(rows + 2 * TAPS, KS * 128),
            f32(tall, group * depth), bf16(tall, group * depth), bf16(tall, group * depth),
            f32(wide, 8 * rows), bf16(wide, 8 * rows), bf16(wide, 8 * rows),
            f32(wide, 256), bf16(wide, 256), bf16(wide, 256),
            bf16(depth, padded + 128), bf16(depth, padded + 128),
            bf16(rows, padded + 128), bf16(rows, padded + 128),
            bf16(32, padded + 128), bf16(32, padded + 128),
            f32(tall, padded), f32(rows, columns + 1024), bf16(256, 128),
        ] + exchange_scratch(nv, rows, width) + exchange_scratch(nv, rows, width) + [
            pltpu.SemaphoreType.DMA((2, half)),
            pltpu.SemaphoreType.DMA((2, half)),
            pltpu.SemaphoreType.DMA((8, chunks)),
            pltpu.SemaphoreType.DMA((4, nv + 1)),
        ],
        compiler_params=pltpu.CompilerParams(
            collective_id=0, has_side_effects=True, vmem_limit_bytes=60 * 1024 * 1024
        ),
        name="whole",
    )(
        pixels, basis_kernels, basis_coeffs[0], row_starts, row_taps[0], col_offsets, col_starts, col_taps[0],
        visit_weights, clip_masks[0], jnp.transpose(decorrelation, (1, 0, 2)),
    )
    return (cleaned[None], template)


def solution(mesh):
    nv, nr = mesh.shape["visit"], mesh.shape["row"]
    return jax.shard_map(
        functools.partial(on_device, nv, nr),
        mesh=mesh,
        in_specs=(
            P("visit", "row", None),
            P(),
            P("visit", None),
            P("visit", "row"),
            P("visit", None, "row"),
            P("visit"),
            P("visit", None),
            P("visit", None, None),
            P("visit"),
            P("visit", "row", None),
            P("visit", None, None),
        ),
        out_specs=(P("visit", "row", None), P("row", "visit")),
        check_vma=False,
    )
```

```python
import functools

import jax
import jax.numpy as jnp
from jax import lax
from jax.experimental import pallas as pl
from jax.experimental.pallas import tpu as pltpu
from jax.sharding import PartitionSpec as P

KS = 21
HALF = KS // 2
TAPS = 8
PAD = 128
CHUNK = 512
F32 = jnp.float32
BF16 = jnp.bfloat16
MESH = pl.DeviceIdType.MESH
VMEM = pl.BlockSpec(memory_space=pltpu.VMEM)
SMEM = pl.BlockSpec(memory_space=pltpu.SMEM)


def padded_width(columns):
    return -(-(columns + 2 * PAD) // CHUNK) * CHUNK


def split(x):
    high = x.astype(BF16)
    low = (x - high.astype(F32)).astype(BF16)
    return high, low


def toeplitz(kernel_t, c, rows, lead):
    line = jnp.broadcast_to(kernel_t[c : c + 1, :], (rows, 128))
    return pltpu.roll(line, lead, 1, stride=1, stride_axis=0)


def kernel_transposed(kernel, square):
    square[...] = jnp.zeros_like(square)
    square[0:KS, 0:KS] = kernel
    return jnp.transpose(square[...])


def piece(high, low, both, partial, start, group, add=False):
    m = both.shape[0]
    window_h = high[:, start : start + CHUNK + 128]
    window_l = low[:, start : start + CHUNK + 128]
    stack_h = [window_h[:, b : b + CHUNK] for b in range(group)]
    stack_l = [window_l[:, b : b + CHUNK] for b in range(group)]
    stack = jnp.concatenate(stack_h + stack_l + stack_h, axis=0)
    total = jnp.dot(both[...], stack, preferred_element_type=F32)
    if add:
        total = total + partial[0:m, start : start + CHUNK]
    partial[0:m, start : start + CHUNK] = total


def shifted_sum(partial, start, rows, group):
    total = jnp.zeros((rows, CHUNK), F32)
    for a in range(-(-KS // group)):
        window = partial[a * rows : (a + 1) * rows, start : start + CHUNK + 2 * PAD]
        shift = PAD + group * a - HALF
        total = total + window[:, shift : shift + CHUNK]
    return total


def store_split(high, low, row, column, values):
    h, l = split(values)
    high[row : row + values.shape[0], column : column + values.shape[1]] = h
    low[row : row + values.shape[0], column : column + values.shape[1]] = l


def store_both(both, values):
    h, l = split(values)
    k = values.shape[1]
    both[:, 0:k] = h
    both[:, k : 2 * k] = h
    both[:, 2 * k : 3 * k] = l


def pack_pair(packed, source, row, columns):
    quarter = columns // 4
    for q in range(4):
        packed[2 * q : 2 * q + 2, :] = source[row : row + 2, q * quarter : (q + 1) * quarter]


def greet(nv, nr):
    v, r = lax.axis_index("visit"), lax.axis_index("row")
    half = nv // 2
    parity, mine = v % 2, v // 2
    barrier = pltpu.get_barrier_semaphore()

    def hello(a, b):
        pl.semaphore_signal(barrier, inc=1, device_id=(a, b), device_id_type=MESH)

    hello(v + 1 - 2 * parity, r)
    for d in range(1, half):
        hello(2 * ((mine + d) % half) + parity, r)

    @pl.when(r > 0)
    def _():
        hello(v, r - 1)

    @pl.when(r < nr - 1)
    def _():
        hello(v, r + 1)


def greeted(nv, nr):
    r = lax.axis_index("row")
    above, below = (r > 0).astype(jnp.int32), (r < nr - 1).astype(jnp.int32)
    pl.semaphore_wait(pltpu.get_barrier_semaphore(), nv // 2 + above + below)


def remote(src, dst, send, recv, device):
    return pltpu.make_async_remote_copy(
        src_ref=src, dst_ref=dst, send_sem=send, recv_sem=recv, device_id=device, device_id_type=MESH
    )


def pair_start(nv, blocks, landed, sems):
    v, r = lax.axis_index("visit"), lax.axis_index("row")
    half = nv // 2
    parity, mine = v % 2, v // 2
    copies = {}
    for d in list(range(1, half)) + [0]:
        k = (mine + d) % half
        copies[d] = remote(
            blocks.at[2 * k + 1 - parity], landed.at[k], sems.at[0, d], sems.at[1, d], (v + 1 - 2 * parity, r)
        )
        copies[d].start()
    return copies


def scatter_sum(nv, blocks, landed, pair_copies, sums, arrived, sems):
    v, r = lax.axis_index("visit"), lax.axis_index("row")
    half = nv // 2
    parity, mine = v % 2, v // 2
    copies = []
    for d in range(1, half):
        k = (mine + d) % half
        pair_copies[d].wait()
        sums[d - 1] = blocks[2 * k + parity] + landed[k]
        copy = remote(sums.at[d - 1], arrived.at[d - 1], sems.at[0, d], sems.at[1, d], (2 * k + parity, r))
        copy.start()
        copies.append(copy)
    pair_copies[0].wait()
    total = blocks[v] + landed[mine]
    for d in range(1, half):
        copies[d - 1].wait()
        total = total + arrived[d - 1]
    return total


def exchange_scratch(nv, rows, width):
    half = nv // 2
    return [
        pltpu.VMEM((half, rows, width), F32),
        pltpu.VMEM((half, rows, width), F32),
        pltpu.VMEM((half, rows, width), F32),
        pltpu.SemaphoreType.DMA((2, half)),
        pltpu.SemaphoreType.DMA((2, half)),
    ]


def whole_kernel(
    nv, nr, science, basis, coeffs, row_starts, row_taps, offsets, col_starts, col_taps, weights, masks, decor,
    cleaned, template,
    shares, numerators, warped, difference, gathered, denominator,
    near_top, near_bottom, packs, pairs_top, pairs_bottom,
    late_top, late_bottom, late_pack_top, late_pack_bottom, late_pair_top, late_pair_bottom,
    square, bands, flat, both, flat_own, own_both, flat_edge, edge_both,
    high, low, second_high, second_low, edge_high, edge_low, partial, shifted, mover,
    d_landed, d_sums, d_arrived, d_pair, d_sum,
    n_landed, n_sums, n_arrived, n_pair, n_sum,
    gather_sems, pass_sems, halo_sems, late_sems,
):
    v, r = lax.axis_index("visit"), lax.axis_index("row")
    rows, columns = science.shape
    width = columns // nv
    half = nv // 2
    parity, mine = v % 2, v // 2
    partner = (v + 1 - 2 * parity, r)
    chunks = packs.shape[1]
    span = columns // chunks
    padded = padded_width(columns)
    depth, group = high.shape[0], 3
    middle = rows + 2 * TAPS

    greet(nv, nr)
    dither = offsets[0]
    for u in range(nv):
        cols = slice(u * width, (u + 1) * width)
        start = col_starts[:, cols] + (lax.broadcasted_iota(jnp.int32, (1, width), 1) + (u * width - dither))
        covered = jnp.where((start >= 0) & (start <= columns - TAPS), weights[0], 0.0)
        shares[u] = masks[:, cols].astype(F32) * covered

    quarter = span // 4
    for n in range(chunks):
        for q in range(4):
            at = n * span + q * quarter
            packs[0, n, 2 * q : 2 * q + 2, :] = science[16:18, at : at + quarter]
            packs[1, n, 2 * q : 2 * q + 2, :] = science[rows - 18 : rows - 16, at : at + quarter]
    greeted(nv, nr)
    up, down = [], []
    for n in range(chunks):
        cols = slice(n * span, (n + 1) * span)
        up.append(remote(science.at[0:16, cols], near_bottom.at[:, cols], halo_sems.at[0, n], halo_sems.at[1, n], (v, r - 1)))
        up.append(remote(packs.at[0, n], pairs_bottom.at[n], halo_sems.at[2, n], halo_sems.at[3, n], (v, r - 1)))
        down.append(remote(science.at[rows - 16 : rows, cols], near_top.at[:, cols], halo_sems.at[4, n], halo_sems.at[5, n], (v, r + 1)))
        down.append(remote(packs.at[1, n], pairs_top.at[n], halo_sems.at[6, n], halo_sems.at[7, n], (v, r + 1)))

    @pl.when(r > 0)
    def _():
        for copy in up:
            copy.start()

    @pl.when(r < nr - 1)
    def _():
        for copy in down:
            copy.start()

    @pl.when(r == 0)
    def _():
        near_top[...] = jnp.zeros_like(near_top)
        pairs_top[...] = jnp.zeros_like(pairs_top)
        late_top[...] = jnp.zeros_like(late_top)
        late_pair_top[...] = jnp.zeros_like(late_pair_top)

    @pl.when(r == nr - 1)
    def _():
        near_bottom[...] = jnp.zeros_like(near_bottom)
        pairs_bottom[...] = jnp.zeros_like(pairs_bottom)
        late_bottom[...] = jnp.zeros_like(late_bottom)
        late_pair_bottom[...] = jnp.zeros_like(late_pair_bottom)

    weight_pairs = pair_start(nv, shares, d_landed, d_pair)

    kernel = coeffs[0] * basis[0]
    for b in range(1, basis.shape[0]):
        kernel = kernel + coeffs[b] * basis[b]
    kernel_t = kernel_transposed(kernel, square)
    m = lax.broadcasted_iota(jnp.int32, (middle, rows), 0) - TAPS
    i = lax.broadcasted_iota(jnp.int32, (middle, rows), 1)
    tap = m - i - row_starts[...]
    inside = (m + r * rows >= 0) & (m + r * rows < nr * rows)
    mix = jnp.zeros((middle, rows), F32)
    for t in range(TAPS):
        mix = mix + jnp.where((tap == t) & inside, row_taps[t : t + 1, :], 0.0)
    for c in range(KS):
        bands[:, c * 128 : (c + 1) * 128] = toeplitz(kernel_t, c, middle, 6)
    folded = lax.dot_general(
        mix, bands[...], (((0,), (0,)), ((), ())), precision=lax.Precision.HIGHEST, preferred_element_type=F32
    )
    flat[...] = jnp.zeros_like(flat)
    for c in range(KS):
        a, b = c // group, c % group
        flat[a * rows : (a + 1) * rows, b * depth : (b + 1) * depth] = folded[:, c * 128 : c * 128 + depth]
    store_both(both, flat[...])

    kernel_t = kernel_transposed(decor[:, 0, :], square)
    flat_own[...] = jnp.zeros_like(flat_own)
    flat_edge[...] = jnp.zeros_like(flat_edge)
    for c in range(KS):
        band = toeplitz(kernel_t, c, rows, 6)
        a, b = c // 8, c % 8
        here = slice(a * rows, (a + 1) * rows)
        flat_own[here, b * rows : (b + 1) * rows] = band[:, 16 : 16 + rows]
        flat_edge[here, b * 32 : b * 32 + 16] = band[:, 0:16]
        flat_edge[here, b * 32 + 16 : b * 32 + 32] = band[:, 16 + rows : 32 + rows]
    store_both(own_both, flat_own[...])
    store_both(edge_both, flat_edge[...])

    for frame in (high, low, second_high, second_low, edge_high, edge_low):
        frame[...] = jnp.zeros_like(frame)
    shifted[...] = jnp.zeros_like(shifted)
    denominator[...] = scatter_sum(nv, shares, d_landed, weight_pairs, d_sums, d_arrived, d_sum)

    tiles = jnp.full((rows, width + 384), dither // 128, jnp.int32)
    place = lax.broadcasted_iota(jnp.int32, (256, 128), 0) - lax.broadcasted_iota(jnp.int32, (256, 128), 1)
    mover[...] = jnp.where(place == 128 - dither % 128, 1.0, 0.0).astype(BF16)

    def warp(u):
        start = u * width
        count = width // 128 + 2
        window = shifted[:, start + 384 : start + 768 + width]
        for t in range(1, 4):
            at = start + 384 - 128 * t
            window = jnp.where(tiles == t, shifted[:, at : at + width + 384], window)
        h, l = split(window)
        stack_h = jnp.concatenate([h[:, 128 * j : 128 * j + 256] for j in range(count)], axis=0)
        stack_l = jnp.concatenate([l[:, 128 * j : 128 * j + 256] for j in range(count)], axis=0)
        moved = jnp.dot(stack_h, mover[...], preferred_element_type=F32)
        moved = moved + jnp.dot(stack_l, mover[...], preferred_element_type=F32)
        window = jnp.concatenate([moved[j * rows : (j + 1) * rows] for j in range(count)], axis=1)
        cols = slice(start, start + width)
        early = col_starts[:, cols] == -3
        taps = [col_taps[t : t + 1, cols] for t in range(TAPS)]
        total = jnp.zeros((rows, width), F32)
        for lag in range(TAPS + 1):
            now = taps[lag] if lag < TAPS else jnp.zeros_like(taps[0])
            before = taps[lag - 1] if lag > 0 else jnp.zeros_like(taps[0])
            at = 128 + lag - 3
            total = total + jnp.where(early, now, before) * window[:, at : at + width]
        warped[:, cols] = total
        numerators[u] = shares[u] * total

    def number_pair(k):
        return remote(numerators.at[2 * k + 1 - parity], n_landed.at[k], n_pair.at[0, k], n_pair.at[1, k], partner)

    def number_sum(k, d):
        return remote(n_sums.at[k], n_arrived.at[d], n_sum.at[0, d], n_sum.at[1, d], (2 * k + parity, r))

    def forward(k):
        number_pair(k).wait()
        n_sums[k] = numerators[2 * k + parity] + n_landed[k]
        d = (k - mine + half) % half

        @pl.when(d > 0)
        def _():
            number_sum(k, d).start()

    pieces = padded // CHUNK
    done_pieces, done_sums, done_warps, done_pairs, done_forwards = 0, 0, 0, 0, 0
    for n in range(chunks):
        cols = slice(n * span, (n + 1) * span)

        @pl.when(r > 0)
        def _():
            down[2 * n].wait_recv()
            down[2 * n + 1].wait_recv()

        @pl.when(r < nr - 1)
        def _():
            up[2 * n].wait_recv()
            up[2 * n + 1].wait_recv()

        store_split(high, low, 24, PAD + n * span, science[:, cols])
        top = near_top[:, cols]
        bottom = near_bottom[:, cols]
        store_split(high, low, 8, PAD + n * span, top)
        store_split(high, low, 24 + rows, PAD + n * span, bottom)
        for q in range(4):
            at = PAD + n * span + q * quarter
            store_split(high, low, 6, at, pairs_top[n, 2 * q : 2 * q + 2, :])
            store_split(high, low, 40 + rows, at, pairs_bottom[n, 2 * q : 2 * q + 2, :])
        last = n == chunks - 1
        while done_pieces < pieces and (last or (done_pieces + 1) * CHUNK + group - PAD <= (n + 1) * span):
            piece(high, low, both, partial, done_pieces * CHUNK, group)
            done_pieces += 1
        while done_sums < columns // CHUNK and done_sums + 2 <= done_pieces:
            start = done_sums * CHUNK
            shifted[:, 640 + start : 640 + start + CHUNK] = shifted_sum(partial, start, rows, group)
            done_sums += 1
        while done_warps < nv and (done_sums * CHUNK >= (done_warps + 1) * width + 8 or done_sums * CHUNK == columns):
            warp(done_warps)
            done_warps += 1
            if done_warps % 2 == 0:
                number_pair(done_pairs).start()
                done_pairs += 1
                if done_pairs >= 2:
                    forward(done_forwards)
                    done_forwards += 1
    while done_forwards < half:
        forward(done_forwards)
        done_forwards += 1

    total = n_sums[mine]
    for d in range(1, half):
        number_sum((mine + d) % half, d).wait()
        total = total + n_arrived[d]
    own = total / jnp.maximum(denominator[...], 1.0)
    template[...] = own
    gathered[v] = own
    sends = []
    for d in range(1, half):
        k = (mine + d) % half
        copy = remote(gathered.at[v], gathered.at[v], gather_sems.at[0, d], gather_sems.at[1, d], (2 * k + parity, r))
        copy.start()
        sends.append(copy)

    def passed(d):
        u = 2 * ((mine + half - d) % half) + parity
        return remote(gathered.at[u], gathered.at[u], pass_sems.at[0, d], pass_sems.at[1, d], partner)

    passes = [passed(d) for d in range(half)]
    passes[0].start()
    ups, downs = [], []

    def subtract(u):
        cols = pl.ds(pl.multiple_of(u * width, width), width)
        at = pl.ds(pl.multiple_of(PAD + u * width, 128), width)
        values = warped[:, cols] - gathered[u]
        difference[:, cols] = values
        h, l = split(values)
        second_high[:, at] = h
        second_low[:, at] = l
        n = len(ups)
        ups.append(remote(difference.at[0:8, cols], late_bottom.at[:, cols], late_sems.at[0, n], late_sems.at[1, n], (v, r - 1)))
        downs.append(
            remote(difference.at[rows - 8 : rows, cols], late_top.at[:, cols], late_sems.at[2, n], late_sems.at[3, n], (v, r + 1))
        )

        @pl.when(r > 0)
        def _():
            ups[-1].start()

        @pl.when(r < nr - 1)
        def _():
            downs[-1].start()

    subtract(v)
    for d in range(half):
        if d > 0:
            sends[d - 1].wait_recv()
            passes[d].start()
            subtract(2 * ((mine + half - d) % half) + parity)
        passes[d].wait_recv()
        subtract(2 * ((mine + half - d) % half) + 1 - parity)
    pack_pair(late_pack_top, difference, 8, columns)
    pack_pair(late_pack_bottom, difference, rows - 10, columns)
    ups.append(remote(late_pack_top, late_pair_bottom, late_sems.at[0, nv], late_sems.at[1, nv], (v, r - 1)))
    downs.append(remote(late_pack_bottom, late_pair_top, late_sems.at[2, nv], late_sems.at[3, nv], (v, r + 1)))

    @pl.when(r > 0)
    def _():
        ups[-1].start()

    @pl.when(r < nr - 1)
    def _():
        downs[-1].start()

    for n in range(pieces):
        piece(second_high, second_low, own_both, partial, n * CHUNK, 8)

    @pl.when(r > 0)
    def _():
        for copy in downs:
            copy.wait_recv()

    @pl.when(r < nr - 1)
    def _():
        for copy in ups:
            copy.wait_recv()

    store_split(edge_high, edge_low, 8, PAD, late_top[...])
    store_split(edge_high, edge_low, 16, PAD, late_bottom[...])
    for q in range(4):
        at = PAD + q * (columns // 4)
        store_split(edge_high, edge_low, 6, at, late_pair_top[2 * q : 2 * q + 2, :])
        store_split(edge_high, edge_low, 24, at, late_pair_bottom[2 * q : 2 * q + 2, :])
    for n in range(pieces):
        piece(edge_high, edge_low, edge_both, partial, n * CHUNK, 8, add=True)
        if n > 0 and n * CHUNK <= columns:
            cleaned[:, (n - 1) * CHUNK : n * CHUNK] = shifted_sum(partial, (n - 1) * CHUNK, rows, 8)

    for copy in sends + passes:
        copy.wait_send()

    @pl.when(r > 0)
    def _():
        for copy in up + ups:
            copy.wait_send()

    @pl.when(r < nr - 1)
    def _():
        for copy in down + downs:
            copy.wait_send()


def hand_over(cleaned, template, cleaned_out, template_out):
    cleaned_out[...] = cleaned[...]
    template_out[...] = template[...]


def shape(*dims):
    return jax.ShapeDtypeStruct(dims, F32)


def on_device(
    nv, nr, science, basis_kernels, basis_coeffs, row_starts, row_taps, col_offsets,
    col_starts, col_taps, visit_weights, clip_masks, decorrelation,
):
    pixels = science[0]
    rows, columns = pixels.shape
    width = columns // nv
    half = nv // 2
    chunks = 4
    span = columns // chunks
    padded = padded_width(columns)
    depth, group = 80, 3
    tall = -(-KS // group) * rows
    wide = -(-KS // 8) * rows
    f32 = lambda *dims: pltpu.VMEM(dims, F32)
    bf16 = lambda *dims: pltpu.VMEM(dims, BF16)
    cleaned, template = pl.pallas_call(
        functools.partial(whole_kernel, nv, nr),
        out_shape=(shape(rows, columns), shape(rows, width)),
        in_specs=[VMEM, VMEM, SMEM, VMEM, VMEM, SMEM, VMEM, VMEM, SMEM, VMEM, VMEM],
        out_specs=(VMEM, VMEM),
        scratch_shapes=[
            f32(nv, rows, width), f32(nv, rows, width), f32(rows, columns), f32(rows, columns),
            f32(nv, rows, width), f32(rows, width),
            f32(16, columns), f32(16, columns), f32(2, chunks, 8, span // 4),
            f32(chunks, 8, span // 4), f32(chunks, 8, span // 4),
            f32(8, columns), f32(8, columns), f32(8, columns // 4), f32(8, columns // 4),
            f32(8, columns // 4), f32(8, columns // 4),
            f32(128, 128), f32(rows + 2 * TAPS, KS * 128),
            f32(tall, group * depth), bf16(tall, 3 * group * depth),
            f32(wide, 8 * rows), bf16(wide, 24 * rows),
            f32(wide, 256), bf16(wide, 768),
            bf16(depth, padded + 128), bf16(depth, padded + 128),
            bf16(rows, padded + 128), bf16(rows, padded + 128),
            bf16(32, padded + 128), bf16(32, padded + 128),
            f32(tall, padded), f32(rows, columns + 1024), bf16(256, 128),
        ] + exchange_scratch(nv, rows, width) + exchange_scratch(nv, rows, width) + [
            pltpu.SemaphoreType.DMA((2, half)),
            pltpu.SemaphoreType.DMA((2, half)),
            pltpu.SemaphoreType.DMA((8, chunks)),
            pltpu.SemaphoreType.DMA((4, nv + 1)),
        ],
        compiler_params=pltpu.CompilerParams(
            collective_id=0, has_side_effects=True, vmem_limit_bytes=60 * 1024 * 1024
        ),
        name="whole",
    )(
        pixels, basis_kernels, basis_coeffs[0], row_starts, row_taps[0], col_offsets, col_starts, col_taps[0],
        visit_weights, clip_masks[0], jnp.transpose(decorrelation, (1, 0, 2)),
    )
    wide_block = pl.BlockSpec((rows, columns // 2), lambda n: (0, n))
    small_block = pl.BlockSpec((rows, width), lambda n: (0, 0))
    cleaned, template = pl.pallas_call(
        hand_over,
        grid=(2,),
        out_shape=(shape(rows, columns), shape(rows, width)),
        in_specs=[wide_block, small_block],
        out_specs=(wide_block, small_block),
        name="hand_over",
    )(cleaned, template)
    return (cleaned[None], template)


def solution(mesh):
    nv, nr = mesh.shape["visit"], mesh.shape["row"]
    return jax.shard_map(
        functools.partial(on_device, nv, nr),
        mesh=mesh,
        in_specs=(
            P("visit", "row", None),
            P(),
            P("visit", None),
            P("visit", "row"),
            P("visit", None, "row"),
            P("visit"),
            P("visit", None),
            P("visit", None, None),
            P("visit"),
            P("visit", "row", None),
            P("visit", None, None),
        ),
        out_specs=(P("visit", "row", None), P("row", "visit")),
        check_vma=False,
    )
```

```python
import functools

import jax
import jax.numpy as jnp
from jax import lax
from jax.experimental import pallas as pl
from jax.experimental.pallas import tpu as pltpu
from jax.sharding import PartitionSpec as P

KS = 21
HALF = KS // 2
TAPS = 8
PAD = 128
CHUNK = 512
F32 = jnp.float32
BF16 = jnp.bfloat16
MESH = pl.DeviceIdType.MESH
VMEM = pl.BlockSpec(memory_space=pltpu.VMEM)
SMEM = pl.BlockSpec(memory_space=pltpu.SMEM)


def padded_width(columns):
    return -(-(columns + 2 * PAD) // CHUNK) * CHUNK


def split(x):
    high = x.astype(BF16)
    low = (x - high.astype(F32)).astype(BF16)
    return high, low


def toeplitz(kernel_t, c, rows, lead):
    line = jnp.broadcast_to(kernel_t[c : c + 1, :], (rows, 128))
    return pltpu.roll(line, lead, 1, stride=1, stride_axis=0)


def kernel_transposed(kernel, square):
    square[...] = jnp.zeros_like(square)
    square[0:KS, 0:KS] = kernel
    return jnp.transpose(square[...])


def piece(high, low, both, partial, start, group, add=False):
    m = both.shape[0]
    window_h = high[:, start : start + CHUNK + 128]
    window_l = low[:, start : start + CHUNK + 128]
    stack_h = [window_h[:, b : b + CHUNK] for b in range(group)]
    stack_l = [window_l[:, b : b + CHUNK] for b in range(group)]
    stack = jnp.concatenate(stack_h + stack_l + stack_h, axis=0)
    total = jnp.dot(both[...], stack, preferred_element_type=F32)
    if add:
        total = total + partial[0:m, start : start + CHUNK]
    partial[0:m, start : start + CHUNK] = total


def shifted_sum(partial, start, rows, group):
    total = jnp.zeros((rows, CHUNK), F32)
    for a in range(-(-KS // group)):
        window = partial[a * rows : (a + 1) * rows, start : start + CHUNK + 2 * PAD]
        shift = PAD + group * a - HALF
        total = total + window[:, shift : shift + CHUNK]
    return total


def store_split(high, low, row, column, values):
    h, l = split(values)
    high[row : row + values.shape[0], column : column + values.shape[1]] = h
    low[row : row + values.shape[0], column : column + values.shape[1]] = l


def store_both(both, values):
    h, l = split(values)
    k = values.shape[1]
    both[:, 0:k] = h
    both[:, k : 2 * k] = h
    both[:, 2 * k : 3 * k] = l


def pack_pair(packed, source, row, columns):
    quarter = columns // 4
    for q in range(4):
        packed[2 * q : 2 * q + 2, :] = source[row : row + 2, q * quarter : (q + 1) * quarter]


def greet(nv, nr):
    v, r = lax.axis_index("visit"), lax.axis_index("row")
    half = nv // 2
    parity, mine = v % 2, v // 2
    barrier = pltpu.get_barrier_semaphore()

    def hello(a, b):
        pl.semaphore_signal(barrier, inc=1, device_id=(a, b), device_id_type=MESH)

    hello(v + 1 - 2 * parity, r)
    for d in range(1, half):
        hello(2 * ((mine + d) % half) + parity, r)

    @pl.when(r > 0)
    def _():
        hello(v, r - 1)

    @pl.when(r < nr - 1)
    def _():
        hello(v, r + 1)


def greeted(nv, nr):
    r = lax.axis_index("row")
    above, below = (r > 0).astype(jnp.int32), (r < nr - 1).astype(jnp.int32)
    pl.semaphore_wait(pltpu.get_barrier_semaphore(), nv // 2 + above + below)


def remote(src, dst, send, recv, device):
    return pltpu.make_async_remote_copy(
        src_ref=src, dst_ref=dst, send_sem=send, recv_sem=recv, device_id=device, device_id_type=MESH
    )


def pair_start(nv, blocks, landed, sems):
    v, r = lax.axis_index("visit"), lax.axis_index("row")
    half = nv // 2
    parity, mine = v % 2, v // 2
    copies = {}
    for d in list(range(1, half)) + [0]:
        k = (mine + d) % half
        copies[d] = remote(
            blocks.at[2 * k + 1 - parity], landed.at[k], sems.at[0, d], sems.at[1, d], (v + 1 - 2 * parity, r)
        )
        copies[d].start()
    return copies


def scatter_start(nv, blocks, landed, pair_copies, sums, arrived, sems):
    v, r = lax.axis_index("visit"), lax.axis_index("row")
    half = nv // 2
    parity, mine = v % 2, v // 2
    copies = []
    for d in range(1, half):
        k = (mine + d) % half
        pair_copies[d].wait()
        sums[d - 1] = blocks[2 * k + parity] + landed[k]
        copy = remote(sums.at[d - 1], arrived.at[d - 1], sems.at[0, d], sems.at[1, d], (2 * k + parity, r))
        copy.start()
        copies.append(copy)
    return copies


def scatter_finish(nv, blocks, landed, pair_copies, arrived, copies):
    v = lax.axis_index("visit")
    half, mine = nv // 2, v // 2
    pair_copies[0].wait()
    total = blocks[v] + landed[mine]
    for d in range(1, half):
        copies[d - 1].wait()
        total = total + arrived[d - 1]
    return total


def exchange_scratch(nv, rows, width):
    half = nv // 2
    return [
        pltpu.VMEM((half, rows, width), F32),
        pltpu.VMEM((half, rows, width), F32),
        pltpu.VMEM((half, rows, width), F32),
        pltpu.SemaphoreType.DMA((2, half)),
        pltpu.SemaphoreType.DMA((2, half)),
    ]


def whole_kernel(
    nv, nr, science, basis, coeffs, row_starts, row_taps, offsets, col_starts, col_taps, weights, masks, decor,
    cleaned, template,
    shares, numerators, warped, difference, gathered, denominator,
    near_top, near_bottom, packs, pairs_top, pairs_bottom,
    late_top, late_bottom, late_pack_top, late_pack_bottom, late_pair_top, late_pair_bottom,
    square, bands, flat, both, flat_own, own_both, flat_edge, edge_both,
    high, low, second_high, second_low, edge_high, edge_low, partial, shifted, mover,
    d_landed, d_sums, d_arrived, d_pair, d_sum,
    n_landed, n_sums, n_arrived, n_pair, n_sum,
    gather_sems, pass_sems, halo_sems, late_sems,
):
    v, r = lax.axis_index("visit"), lax.axis_index("row")
    rows, columns = science.shape
    width = columns // nv
    half = nv // 2
    parity, mine = v % 2, v // 2
    partner = (v + 1 - 2 * parity, r)
    chunks = packs.shape[1]
    span = columns // chunks
    padded = padded_width(columns)
    depth, group = high.shape[0], 3
    middle = rows + 2 * TAPS

    greet(nv, nr)
    dither = offsets[0]
    for u in range(nv):
        cols = slice(u * width, (u + 1) * width)
        start = col_starts[:, cols] + (lax.broadcasted_iota(jnp.int32, (1, width), 1) + (u * width - dither))
        covered = jnp.where((start >= 0) & (start <= columns - TAPS), weights[0], 0.0)
        shares[u] = masks[:, cols].astype(F32) * covered

    quarter = span // 4
    for n in range(chunks):
        for q in range(4):
            at = n * span + q * quarter
            packs[0, n, 2 * q : 2 * q + 2, :] = science[16:18, at : at + quarter]
            packs[1, n, 2 * q : 2 * q + 2, :] = science[rows - 18 : rows - 16, at : at + quarter]
    greeted(nv, nr)
    up, down = [], []
    for n in range(chunks):
        cols = slice(n * span, (n + 1) * span)
        up.append(remote(science.at[0:16, cols], near_bottom.at[:, cols], halo_sems.at[0, n], halo_sems.at[1, n], (v, r - 1)))
        up.append(remote(packs.at[0, n], pairs_bottom.at[n], halo_sems.at[2, n], halo_sems.at[3, n], (v, r - 1)))
        down.append(remote(science.at[rows - 16 : rows, cols], near_top.at[:, cols], halo_sems.at[4, n], halo_sems.at[5, n], (v, r + 1)))
        down.append(remote(packs.at[1, n], pairs_top.at[n], halo_sems.at[6, n], halo_sems.at[7, n], (v, r + 1)))

    @pl.when(r > 0)
    def _():
        for copy in up:
            copy.start()

    @pl.when(r < nr - 1)
    def _():
        for copy in down:
            copy.start()

    @pl.when(r == 0)
    def _():
        near_top[...] = jnp.zeros_like(near_top)
        pairs_top[...] = jnp.zeros_like(pairs_top)
        late_top[...] = jnp.zeros_like(late_top)
        late_pair_top[...] = jnp.zeros_like(late_pair_top)

    @pl.when(r == nr - 1)
    def _():
        near_bottom[...] = jnp.zeros_like(near_bottom)
        pairs_bottom[...] = jnp.zeros_like(pairs_bottom)
        late_bottom[...] = jnp.zeros_like(late_bottom)
        late_pair_bottom[...] = jnp.zeros_like(late_pair_bottom)

    weight_pairs = pair_start(nv, shares, d_landed, d_pair)

    kernel = coeffs[0] * basis[0]
    for b in range(1, basis.shape[0]):
        kernel = kernel + coeffs[b] * basis[b]
    kernel_t = kernel_transposed(kernel, square)
    m = lax.broadcasted_iota(jnp.int32, (middle, rows), 0) - TAPS
    i = lax.broadcasted_iota(jnp.int32, (middle, rows), 1)
    tap = m - i - row_starts[...]
    inside = (m + r * rows >= 0) & (m + r * rows < nr * rows)
    mix = jnp.zeros((middle, rows), F32)
    for t in range(TAPS):
        mix = mix + jnp.where((tap == t) & inside, row_taps[t : t + 1, :], 0.0)
    for c in range(KS):
        bands[:, c * 128 : (c + 1) * 128] = toeplitz(kernel_t, c, middle, 6)
    folded = lax.dot_general(
        mix, bands[...], (((0,), (0,)), ((), ())), precision=lax.Precision.HIGHEST, preferred_element_type=F32
    )
    flat[...] = jnp.zeros_like(flat)
    for c in range(KS):
        a, b = c // group, c % group
        flat[a * rows : (a + 1) * rows, b * depth : (b + 1) * depth] = folded[:, c * 128 : c * 128 + depth]
    store_both(both, flat[...])

    weight_sums = scatter_start(nv, shares, d_landed, weight_pairs, d_sums, d_arrived, d_sum)

    kernel_t = kernel_transposed(decor[:, 0, :], square)
    flat_own[...] = jnp.zeros_like(flat_own)
    flat_edge[...] = jnp.zeros_like(flat_edge)
    for c in range(KS):
        band = toeplitz(kernel_t, c, rows, 6)
        a, b = c // 8, c % 8
        here = slice(a * rows, (a + 1) * rows)
        flat_own[here, b * rows : (b + 1) * rows] = band[:, 16 : 16 + rows]
        flat_edge[here, b * 32 : b * 32 + 16] = band[:, 0:16]
        flat_edge[here, b * 32 + 16 : b * 32 + 32] = band[:, 16 + rows : 32 + rows]
    store_both(own_both, flat_own[...])
    store_both(edge_both, flat_edge[...])

    for frame in (high, low, second_high, second_low, edge_high, edge_low):
        frame[...] = jnp.zeros_like(frame)
    shifted[...] = jnp.zeros_like(shifted)

    tiles = jnp.full((rows, width + 384), dither // 128, jnp.int32)
    place = lax.broadcasted_iota(jnp.int32, (256, 128), 0) - lax.broadcasted_iota(jnp.int32, (256, 128), 1)
    mover[...] = jnp.where(place == 128 - dither % 128, 1.0, 0.0).astype(BF16)

    def warp(u):
        start = u * width
        count = width // 128 + 2
        window = shifted[:, start + 384 : start + 768 + width]
        for t in range(1, 4):
            at = start + 384 - 128 * t
            window = jnp.where(tiles == t, shifted[:, at : at + width + 384], window)
        h, l = split(window)
        stack_h = jnp.concatenate([h[:, 128 * j : 128 * j + 256] for j in range(count)], axis=0)
        stack_l = jnp.concatenate([l[:, 128 * j : 128 * j + 256] for j in range(count)], axis=0)
        moved = jnp.dot(stack_h, mover[...], preferred_element_type=F32)
        moved = moved + jnp.dot(stack_l, mover[...], preferred_element_type=F32)
        window = jnp.concatenate([moved[j * rows : (j + 1) * rows] for j in range(count)], axis=1)
        cols = slice(start, start + width)
        early = col_starts[:, cols] == -3
        taps = [col_taps[t : t + 1, cols] for t in range(TAPS)]
        total = jnp.zeros((rows, width), F32)
        for lag in range(TAPS + 1):
            now = taps[lag] if lag < TAPS else jnp.zeros_like(taps[0])
            before = taps[lag - 1] if lag > 0 else jnp.zeros_like(taps[0])
            at = 128 + lag - 3
            total = total + jnp.where(early, now, before) * window[:, at : at + width]
        warped[:, cols] = total
        numerators[u] = shares[u] * total

    def number_pair(k):
        return remote(numerators.at[2 * k + 1 - parity], n_landed.at[k], n_pair.at[0, k], n_pair.at[1, k], partner)

    def number_sum(k, d):
        return remote(n_sums.at[k], n_arrived.at[d], n_sum.at[0, d], n_sum.at[1, d], (2 * k + parity, r))

    def forward(k):
        number_pair(k).wait()
        n_sums[k] = numerators[2 * k + parity] + n_landed[k]
        d = (k - mine + half) % half

        @pl.when(d > 0)
        def _():
            number_sum(k, d).start()

    pieces = padded // CHUNK
    done_pieces, done_sums, done_warps, done_pairs, done_forwards = 0, 0, 0, 0, 0
    for n in range(chunks):
        cols = slice(n * span, (n + 1) * span)

        @pl.when(r > 0)
        def _():
            down[2 * n].wait_recv()
            down[2 * n + 1].wait_recv()

        @pl.when(r < nr - 1)
        def _():
            up[2 * n].wait_recv()
            up[2 * n + 1].wait_recv()

        store_split(high, low, 24, PAD + n * span, science[:, cols])
        top = near_top[:, cols]
        bottom = near_bottom[:, cols]
        store_split(high, low, 8, PAD + n * span, top)
        store_split(high, low, 24 + rows, PAD + n * span, bottom)
        for q in range(4):
            at = PAD + n * span + q * quarter
            store_split(high, low, 6, at, pairs_top[n, 2 * q : 2 * q + 2, :])
            store_split(high, low, 40 + rows, at, pairs_bottom[n, 2 * q : 2 * q + 2, :])
        last = n == chunks - 1
        while done_pieces < pieces and (last or (done_pieces + 1) * CHUNK + group - PAD <= (n + 1) * span):
            piece(high, low, both, partial, done_pieces * CHUNK, group)
            done_pieces += 1
        while done_sums < columns // CHUNK and done_sums + 2 <= done_pieces:
            start = done_sums * CHUNK
            shifted[:, 640 + start : 640 + start + CHUNK] = shifted_sum(partial, start, rows, group)
            done_sums += 1
        while done_warps < nv and (done_sums * CHUNK >= (done_warps + 1) * width + 8 or done_sums * CHUNK == columns):
            warp(done_warps)
            done_warps += 1
            if done_warps % 2 == 0:
                number_pair(done_pairs).start()
                done_pairs += 1
                if done_pairs >= 2:
                    forward(done_forwards)
                    done_forwards += 1
    while done_forwards < half:
        forward(done_forwards)
        done_forwards += 1
    denominator[...] = scatter_finish(nv, shares, d_landed, weight_pairs, d_arrived, weight_sums)

    total = n_sums[mine]
    for d in range(1, half):
        number_sum((mine + d) % half, d).wait()
        total = total + n_arrived[d]
    own = total / jnp.maximum(denominator[...], 1.0)
    template[...] = own
    gathered[v] = own
    sends = []
    for d in range(1, half):
        k = (mine + d) % half
        copy = remote(gathered.at[v], gathered.at[v], gather_sems.at[0, d], gather_sems.at[1, d], (2 * k + parity, r))
        copy.start()
        sends.append(copy)

    def passed(d):
        u = 2 * ((mine + half - d) % half) + parity
        return remote(gathered.at[u], gathered.at[u], pass_sems.at[0, d], pass_sems.at[1, d], partner)

    passes = [passed(d) for d in range(half)]
    passes[0].start()
    ups, downs = [], []

    def subtract(u):
        cols = pl.ds(pl.multiple_of(u * width, width), width)
        at = pl.ds(pl.multiple_of(PAD + u * width, 128), width)
        values = warped[:, cols] - gathered[u]
        difference[:, cols] = values
        h, l = split(values)
        second_high[:, at] = h
        second_low[:, at] = l
        n = len(ups)
        ups.append(remote(difference.at[0:8, cols], late_bottom.at[:, cols], late_sems.at[0, n], late_sems.at[1, n], (v, r - 1)))
        downs.append(
            remote(difference.at[rows - 8 : rows, cols], late_top.at[:, cols], late_sems.at[2, n], late_sems.at[3, n], (v, r + 1))
        )

        @pl.when(r > 0)
        def _():
            ups[-1].start()

        @pl.when(r < nr - 1)
        def _():
            downs[-1].start()

    subtract(v)
    for d in range(half):
        if d > 0:
            sends[d - 1].wait_recv()
            passes[d].start()
            subtract(2 * ((mine + half - d) % half) + parity)
        passes[d].wait_recv()
        subtract(2 * ((mine + half - d) % half) + 1 - parity)
    pack_pair(late_pack_top, difference, 8, columns)
    pack_pair(late_pack_bottom, difference, rows - 10, columns)
    ups.append(remote(late_pack_top, late_pair_bottom, late_sems.at[0, nv], late_sems.at[1, nv], (v, r - 1)))
    downs.append(remote(late_pack_bottom, late_pair_top, late_sems.at[2, nv], late_sems.at[3, nv], (v, r + 1)))

    @pl.when(r > 0)
    def _():
        ups[-1].start()

    @pl.when(r < nr - 1)
    def _():
        downs[-1].start()

    for n in range(pieces):
        piece(second_high, second_low, own_both, partial, n * CHUNK, 8)

    @pl.when(r > 0)
    def _():
        for copy in downs:
            copy.wait_recv()

    @pl.when(r < nr - 1)
    def _():
        for copy in ups:
            copy.wait_recv()

    store_split(edge_high, edge_low, 8, PAD, late_top[...])
    store_split(edge_high, edge_low, 16, PAD, late_bottom[...])
    for q in range(4):
        at = PAD + q * (columns // 4)
        store_split(edge_high, edge_low, 6, at, late_pair_top[2 * q : 2 * q + 2, :])
        store_split(edge_high, edge_low, 24, at, late_pair_bottom[2 * q : 2 * q + 2, :])
    for n in range(pieces):
        piece(edge_high, edge_low, edge_both, partial, n * CHUNK, 8, add=True)
        if n > 0 and n * CHUNK <= columns:
            cleaned[:, (n - 1) * CHUNK : n * CHUNK] = shifted_sum(partial, (n - 1) * CHUNK, rows, 8)

    for copy in sends + passes:
        copy.wait_send()

    @pl.when(r > 0)
    def _():
        for copy in up + ups:
            copy.wait_send()

    @pl.when(r < nr - 1)
    def _():
        for copy in down + downs:
            copy.wait_send()


def hand_over(cleaned, template, cleaned_out, template_out):
    cleaned_out[...] = cleaned[...]
    template_out[...] = template[...]


def shape(*dims):
    return jax.ShapeDtypeStruct(dims, F32)


def on_device(
    nv, nr, science, basis_kernels, basis_coeffs, row_starts, row_taps, col_offsets,
    col_starts, col_taps, visit_weights, clip_masks, decorrelation,
):
    pixels = science[0]
    rows, columns = pixels.shape
    width = columns // nv
    half = nv // 2
    chunks = 4
    span = columns // chunks
    padded = padded_width(columns)
    depth, group = 80, 3
    tall = -(-KS // group) * rows
    wide = -(-KS // 8) * rows
    f32 = lambda *dims: pltpu.VMEM(dims, F32)
    bf16 = lambda *dims: pltpu.VMEM(dims, BF16)
    cleaned, template = pl.pallas_call(
        functools.partial(whole_kernel, nv, nr),
        out_shape=(shape(rows, columns), shape(rows, width)),
        in_specs=[VMEM, VMEM, SMEM, VMEM, VMEM, SMEM, VMEM, VMEM, SMEM, VMEM, VMEM],
        out_specs=(VMEM, VMEM),
        scratch_shapes=[
            f32(nv, rows, width), f32(nv, rows, width), f32(rows, columns), f32(rows, columns),
            f32(nv, rows, width), f32(rows, width),
            f32(16, columns), f32(16, columns), f32(2, chunks, 8, span // 4),
            f32(chunks, 8, span // 4), f32(chunks, 8, span // 4),
            f32(8, columns), f32(8, columns), f32(8, columns // 4), f32(8, columns // 4),
            f32(8, columns // 4), f32(8, columns // 4),
            f32(128, 128), f32(rows + 2 * TAPS, KS * 128),
            f32(tall, group * depth), bf16(tall, 3 * group * depth),
            f32(wide, 8 * rows), bf16(wide, 24 * rows),
            f32(wide, 256), bf16(wide, 768),
            bf16(depth, padded + 128), bf16(depth, padded + 128),
            bf16(rows, padded + 128), bf16(rows, padded + 128),
            bf16(32, padded + 128), bf16(32, padded + 128),
            f32(tall, padded), f32(rows, columns + 1024), bf16(256, 128),
        ] + exchange_scratch(nv, rows, width) + exchange_scratch(nv, rows, width) + [
            pltpu.SemaphoreType.DMA((2, half)),
            pltpu.SemaphoreType.DMA((2, half)),
            pltpu.SemaphoreType.DMA((8, chunks)),
            pltpu.SemaphoreType.DMA((4, nv + 1)),
        ],
        compiler_params=pltpu.CompilerParams(
            collective_id=0, has_side_effects=True, vmem_limit_bytes=60 * 1024 * 1024
        ),
        name="whole",
    )(
        pixels, basis_kernels, basis_coeffs[0], row_starts, row_taps[0], col_offsets, col_starts, col_taps[0],
        visit_weights, clip_masks[0], jnp.transpose(decorrelation, (1, 0, 2)),
    )
    wide_block = pl.BlockSpec((rows, columns // 2), lambda n: (0, n))
    small_block = pl.BlockSpec((rows, width), lambda n: (0, 0))
    cleaned, template = pl.pallas_call(
        hand_over,
        grid=(2,),
        out_shape=(shape(rows, columns), shape(rows, width)),
        in_specs=[wide_block, small_block],
        out_specs=(wide_block, small_block),
        name="hand_over",
    )(cleaned, template)
    return (cleaned[None], template)


def solution(mesh):
    nv, nr = mesh.shape["visit"], mesh.shape["row"]
    return jax.shard_map(
        functools.partial(on_device, nv, nr),
        mesh=mesh,
        in_specs=(
            P("visit", "row", None),
            P(),
            P("visit", None),
            P("visit", "row"),
            P("visit", None, "row"),
            P("visit"),
            P("visit", None),
            P("visit", None, None),
            P("visit"),
            P("visit", "row", None),
            P("visit", None, None),
        ),
        out_specs=(P("visit", "row", None), P("row", "visit")),
        check_vma=False,
    )
```
